256 devices in a mesh: row: 4 (over z_lo, core), col: 64 (over y, z_hi, x).
Axes of the slice: x: 4, y: 4, z: 8 (z_hi: 4, z_lo: 2; z = z_hi * 2 + z_lo), core: 2. Of those that a mesh axis runs over, the one named last changes fastest.
Arguments:
- tokens: bfloat16 [1024, 8192], P('col', 'row'), may hold values from -6 to 6
- out_grad: bfloat16 [1024, 8192], P('col', 'row'), may hold values from -2 to 2
- gate_weight: bfloat16 [8192, 28672], P('row', 'col'), may hold values from -0.0625 to 0.0625
- up_weight: bfloat16 [8192, 28672], P('row', 'col'), may hold values from -0.0625 to 0.0625
- down_weight: bfloat16 [28672, 8192], P('col', 'row'), may hold values from -0.03125 to 0.03125
Outputs:
- grad_input: bfloat16 [1024, 8192], P('col', 'row')
- grad_gate: bfloat16 [8192, 28672], P('row', 'col')
- grad_up: bfloat16 [8192, 28672], P('row', 'col')
- grad_down: bfloat16 [28672, 8192], P('col', 'row')
The draws below stay inside these ranges and needn't reach their ends.
All inputs are finite; a program needn't handle non-finite values.
Results may differ from the reference program's by a relative error of at most 0.005.
Values may be sent and summed in bfloat16 or wider, within the bound.
No kernel may reach another device: no remote copies, remote signals or barrier semaphores. Data moves between devices by JAX's collectives and lax.ppermute only.
A program may use at most 128 MiB of HBM per device.

```python
import jax
import jax.numpy as jnp
from jax import lax

D = 8192
FF = 28672
TOKENS = 1024
N_COL = 64


def block_scale(key, extent, shards, smallest, high):
    def one(position, blocks):
        steps = jax.random.uniform(jax.random.fold_in(jax.random.fold_in(key, 6), position), (blocks,), jnp.float32, smallest / len(shards), high / len(shards))
        return jnp.repeat(jnp.exp(steps), extent[position] // blocks).reshape((-1,) + (1,) * (len(extent) - position - 1))

    loudness = one(*shards[0])
    for cut in shards[1:]:
        loudness = loudness * one(*cut)
    return loudness


def gaussian(own_key, dims, deviation, most, shards=(), held_as=jnp.bfloat16):
    result = deviation * jax.random.normal(own_key, dims, jnp.float32)
    if shards:
        result = result * block_scale(own_key, dims, shards, -0.22, 0.18)
    return jnp.clip(result, -most, most).astype(held_as)


def setup_inputs(seed: int = 0) -> dict:
    key_list = jax.random.split(jax.random.key(seed), 6)
    tokens = gaussian(key_list[0], (TOKENS, D), 1.0, 6.0, ((0, 64), (1, 4)))
    out_grad = gaussian(key_list[1], (TOKENS, D), 0.15, 2.0, ((0, 64), (1, 4)))
    gate_weight = gaussian(key_list[2], (D, FF), D ** -0.5, 0.0625, ((0, 4), (1, 64)))
    up_weight = gaussian(key_list[3], (D, FF), D ** -0.5, 0.0625, ((0, 4), (1, 64)))
    down_weight = gaussian(key_list[4], (FF, D), FF ** -0.5, 0.03125, ((0, 64), (1, 4)))
    return dict(tokens=tokens, out_grad=out_grad, gate_weight=gate_weight, up_weight=up_weight, down_weight=down_weight)


def pointwise(gate, up, hidden_grad):
    logistic = jax.nn.sigmoid(gate)
    active = gate * logistic
    hidden = (active * up).astype(jnp.bfloat16)
    d_gate = (hidden_grad * up * logistic * (1.0 + gate * (1.0 - logistic))).astype(jnp.bfloat16)
    d_up = (hidden_grad * active).astype(jnp.bfloat16)
    return hidden, d_gate, d_up


def reference(tokens, out_grad, gate_weight, up_weight, down_weight):
    width = FF // N_COL
    gate_blocks = gate_weight.reshape(D, N_COL, width).transpose(1, 0, 2)
    up_blocks = up_weight.reshape(D, N_COL, width).transpose(1, 0, 2)
    down_blocks = down_weight.reshape(N_COL, width, D)

    def step(carry, pieces):
        gate_piece, up_piece, down_piece = pieces
        gate = jnp.dot(tokens, gate_piece, preferred_element_type=jnp.float32)
        up = jnp.dot(tokens, up_piece, preferred_element_type=jnp.float32)
        hidden_grad = jnp.dot(out_grad, down_piece.T, preferred_element_type=jnp.float32)
        hidden, d_gate, d_up = pointwise(gate, up, hidden_grad)
        grad_down = jnp.dot(hidden.T, out_grad, preferred_element_type=jnp.float32).astype(jnp.bfloat16)
        grad_gate = jnp.dot(tokens.T, d_gate, preferred_element_type=jnp.float32).astype(jnp.bfloat16)
        grad_up = jnp.dot(tokens.T, d_up, preferred_element_type=jnp.float32).astype(jnp.bfloat16)
        carry = carry + jnp.dot(d_gate, gate_piece.T, preferred_element_type=jnp.float32)
        carry = carry + jnp.dot(d_up, up_piece.T, preferred_element_type=jnp.float32)
        return carry, (grad_gate, grad_up, grad_down)

    initial = jnp.zeros((TOKENS, D), jnp.float32)
    total, stacked = lax.scan(step, initial, (gate_blocks, up_blocks, down_blocks))
    grad_gate = stacked[0].transpose(1, 0, 2).reshape(D, FF)
    grad_up = stacked[1].transpose(1, 0, 2).reshape(D, FF)
    grad_down = stacked[2].reshape(FF, D)
    return total.astype(jnp.bfloat16), grad_gate, grad_up, grad_down
```

```python
import jax
import jax.numpy as jnp
from jax import lax
from jax.sharding import PartitionSpec as P

BF = jnp.bfloat16
F32 = jnp.float32


def shift(value, axis, amount):
    def moved(c):
        y, z, x = c // 16, (c // 4) % 4, c % 4
        if axis == "y":
            y = (y + amount) % 4
        elif axis == "z":
            z = (z + amount) % 4
        else:
            x = (x + amount) % 4
        return y * 16 + z * 4 + x

    return lax.ppermute(value, "col", [(c, moved(c)) for c in range(64)])


def swap_core(value):
    return lax.ppermute(value, "row", [(r, r ^ 1) for r in range(4)])


def swap_chip(value):
    return lax.ppermute(value, "row", [(r, r ^ 2) for r in range(4)])


def contract(left, right, left_dim, right_dim):
    return lax.dot_general(
        left, right, (((left_dim,), (right_dim,)), ((), ())), preferred_element_type=F32
    )


def pointwise(gate, up, hidden_grad):
    logistic = jax.nn.sigmoid(gate)
    active = gate * logistic
    hidden = (active * up).astype(BF)
    d_gate = (hidden_grad * up * logistic * (1.0 + gate * (1.0 - logistic))).astype(BF)
    d_up = (hidden_grad * active).astype(BF)
    return hidden, d_gate, d_up


def gather_block(parts, axis):
    pieces = [parts] + [shift(parts, axis, -k) for k in (1, 2, 3)]
    return jnp.stack(pieces, axis=1)


def gather_last(own_x, own_g, axis):
    x_down = shift(own_x, axis, 1)
    g_up = shift(own_g, axis, -1)
    g_down = shift(own_g, axis, 1)
    x_up = shift(own_x, axis, -1)
    x_far = shift(x_down, axis, 1)
    g_far = shift(g_up, axis, -1)
    return {0: (own_x, own_g), -1: (x_down, g_down), 1: (x_up, g_up), 2: (x_far, g_far)}


def scatter_first(blocks, axis):
    total = blocks[0]
    for k in (1, -1, 2):
        total = total + shift(blocks[k].astype(BF), axis, k).astype(F32)
    return total


def scatter(total, axis):
    rows = total.shape[0] // 4
    result = total[:rows]
    for k in (1, 3, 2):
        result = result + shift(total[k * rows:(k + 1) * rows].astype(BF), axis, k).astype(F32)
    return result


def local(tokens, out_grad, gate_weight, up_weight, down_weight):
    width, hidden_units = gate_weight.shape
    half = hidden_units // 2
    core = lax.axis_index("row") % 2

    def halves(weight, dim):
        keep = lax.dynamic_slice_in_dim(weight, core * half, half, dim)
        send = lax.dynamic_slice_in_dim(weight, (1 - core) * half, half, dim)
        return keep, send

    gate_keep, gate_send = halves(gate_weight, 1)
    up_keep, up_send = halves(up_weight, 1)
    down_keep, down_send = halves(down_weight, 0)
    pair_keep = jnp.concatenate([gate_keep, up_keep], axis=1)
    pair_send = jnp.concatenate([gate_send, up_send], axis=1)

    rows = tokens.shape[0] // 2
    both = jnp.stack([tokens, out_grad])
    slabs = [both] + [shift(both, "z", -k) for k in (1, 2, 3)]
    blocks = {}
    for stream, (first, last) in enumerate((("x", "y"), ("y", "x"))):
        parts = jnp.stack([slab[:, stream * rows:(stream + 1) * rows] for slab in slabs], axis=1)
        whole = gather_block(parts, first).reshape(2, 16 * rows, width)
        blocks[stream] = gather_last(whole[0], whole[1], last)
    size = 16 * rows

    groups = [[(0, 0), (1, 0)], [(0, -1), (0, 1), (1, -1), (1, 1)], [(0, 2), (1, 2)]]
    xs, gs, hiddens, d_gates, d_ups = [], [], [], [], []
    partial = {0: {}, 1: {}}
    for group in groups:
        x = jnp.concatenate([blocks[s][k][0] for s, k in group])
        g = jnp.concatenate([blocks[s][k][1] for s, k in group])
        send_pair = contract(pair_send, x, 0, 1)
        send_grad = contract(down_send, g, 1, 1)
        got_pair = swap_core(send_pair)
        got_grad = swap_core(send_grad)
        sum_pair = contract(pair_keep, x, 0, 1) + got_pair
        sum_grad = contract(down_keep, g, 1, 1) + got_grad
        sums = jnp.concatenate([sum_pair, sum_grad])
        sums = sums + swap_chip(sums.astype(BF)).astype(F32)
        hidden, d_gate, d_up = pointwise(sums[:half], sums[half:2 * half], sums[2 * half:])
        mine = jnp.concatenate([d_gate, d_up, hidden])
        other = swap_core(mine)
        gradient = contract(mine[:2 * half], pair_keep, 0, 1) + contract(other[:2 * half], pair_send, 0, 1)
        for i, (s, k) in enumerate(group):
            partial[s][k] = gradient[i * size:(i + 1) * size]
        low = jnp.where(core == 0, mine, other)
        high = jnp.where(core == 0, other, mine)
        d_gates.append(jnp.concatenate([low[:half], high[:half]]))
        d_ups.append(jnp.concatenate([low[half:2 * half], high[half:2 * half]]))
        hiddens.append(jnp.concatenate([low[2 * half:], high[2 * half:]]))
        xs.append(x)
        gs.append(g)

    results = []
    for stream, order in enumerate((("y", "x"), ("x", "y"))):
        total = scatter_first(partial[stream], order[0])
        total = scatter(total, order[1])
        results.append(scatter(total, "z"))
    grad_input = jnp.concatenate(results).astype(BF)

    all_x = jnp.concatenate(xs)
    all_g = jnp.concatenate(gs)
    grad_gate = contract(jnp.concatenate(d_gates, axis=1), all_x, 1, 0).astype(BF).T
    grad_up = contract(jnp.concatenate(d_ups, axis=1), all_x, 1, 0).astype(BF).T
    grad_down = contract(jnp.concatenate(hiddens, axis=1), all_g, 1, 0).astype(BF)
    return (grad_input, grad_gate, grad_up, grad_down)


def solution(mesh):
    in_specs = (P("col", "row"), P("col", "row"), P("row", "col"), P("row", "col"), P("col", "row"))
    out_specs = (P("col", "row"), P("row", "col"), P("row", "col"), P("col", "row"))
    return jax.shard_map(local, mesh=mesh, in_specs=in_specs, out_specs=out_specs, check_vma=False)
```

```python
import jax
import jax.numpy as jnp
from jax import lax
from jax.sharding import PartitionSpec as P

BF = jnp.bfloat16
F32 = jnp.float32


def shift(value, axis, amount):
    def moved(c):
        y, z, x = c // 16, (c // 4) % 4, c % 4
        if axis == "y":
            y = (y + amount) % 4
        elif axis == "z":
            z = (z + amount) % 4
        else:
            x = (x + amount) % 4
        return y * 16 + z * 4 + x

    return lax.ppermute(value, "col", [(c, moved(c)) for c in range(64)])


def swap_core(value):
    return lax.ppermute(value, "row", [(r, r ^ 1) for r in range(4)])


def swap_chip(value):
    return lax.ppermute(value, "row", [(r, r ^ 2) for r in range(4)])


def contract(left, right, left_dim, right_dim):
    return lax.dot_general(
        left, right, (((left_dim,), (right_dim,)), ((), ())), preferred_element_type=F32
    )


def pointwise(gate, up, hidden_grad):
    logistic = jax.nn.sigmoid(gate)
    active = gate * logistic
    hidden = (active * up).astype(BF)
    d_gate = (hidden_grad * up * logistic * (1.0 + gate * (1.0 - logistic))).astype(BF)
    d_up = (hidden_grad * active).astype(BF)
    return hidden, d_gate, d_up


def gather_block(parts, axis):
    pieces = [parts] + [shift(parts, axis, -k) for k in (1, 2, 3)]
    return jnp.stack(pieces, axis=1)


def gather_last(own, axis):
    down = shift(own, axis, 1)
    up = shift(own, axis, -1)
    far = (shift(down[0], axis, 1), shift(up[1], axis, -1))
    return {0: (own[0], own[1]), -1: (down[0], down[1]), 1: (up[0], up[1]), 2: far}


def scatter_first(blocks, axis):
    total = blocks[0]
    for k in (1, -1, 2):
        total = total + shift(blocks[k], axis, k).astype(F32)
    return total


def scatter(total, axis):
    rows = total.shape[0] // 4
    result = total[:rows]
    for k in (1, 3, 2):
        result = result + shift(total[k * rows:(k + 1) * rows].astype(BF), axis, k).astype(F32)
    return result


def scatter_slabs(totals):
    rows = totals[0].shape[0] // 4
    pieces = [jnp.concatenate([t[k * rows:(k + 1) * rows] for t in totals]) for k in range(4)]
    result = pieces[0]
    for k in (1, 3, 2):
        result = result + shift(pieces[k], "z", k)
    return result


def after(values, earlier):
    return lax.optimization_barrier((values, earlier))[0]


def local(tokens, out_grad, gate_weight, up_weight, down_weight):
    width, hidden_units = gate_weight.shape
    half = hidden_units // 2
    core = lax.axis_index("row") % 2

    def halves(weight, dim):
        keep = lax.dynamic_slice_in_dim(weight, core * half, half, dim)
        send = lax.dynamic_slice_in_dim(weight, (1 - core) * half, half, dim)
        return keep, send

    gate_keep, gate_send = halves(gate_weight, 1)
    up_keep, up_send = halves(up_weight, 1)
    down_keep, down_send = halves(down_weight, 0)
    pair_keep = jnp.concatenate([gate_keep, up_keep], axis=1)
    pair_send = jnp.concatenate([gate_send, up_send], axis=1)

    rows = tokens.shape[0] // 2
    both = jnp.stack([tokens, out_grad])
    slabs = [both] + [shift(both, "z", -k) for k in (1, 2, 3)]
    slabs, weights = lax.optimization_barrier((slabs, (pair_keep, pair_send, down_keep, down_send)))
    pair_keep, pair_send, down_keep, down_send = weights
    blocks = {}
    for stream, (first, last) in enumerate((("x", "y"), ("y", "x"))):
        parts = jnp.stack([slab[:, stream * rows:(stream + 1) * rows] for slab in slabs], axis=1)
        whole = gather_block(parts, first).reshape(2, 16 * rows, width)
        blocks[stream] = gather_last(whole, last)
    size = 16 * rows

    groups = [[(0, 0), (1, 0)], [(1, -1), (1, 1)], [(0, -1), (0, 1)], [(0, 2), (1, 2)]]
    xs, gs, hiddens, d_gates, d_ups = [], [], [], [], []
    partial = {0: {}, 1: {}}
    states = []
    for group in groups:
        x = jnp.concatenate([blocks[s][k][0] for s, k in group])
        g = jnp.concatenate([blocks[s][k][1] for s, k in group])
        if states:
            x, g = after((x, g), states[-1][1])
        xs.append(x)
        gs.append(g)
        got_pair = swap_core(contract(pair_send, x, 0, 1))
        got_grad = swap_core(contract(down_send, g, 1, 1))
        sum_pair = contract(pair_keep, x, 0, 1) + got_pair
        sum_grad = contract(down_keep, g, 1, 1) + got_grad
        sums = jnp.concatenate([sum_pair, sum_grad])
        states.append([sums, sums.astype(BF)])
    for group, (sums, sent) in zip(groups, states):
        sums = sums + swap_chip(sent).astype(F32)
        hidden, d_gate, d_up = pointwise(sums[:half], sums[half:2 * half], sums[2 * half:])
        mine = jnp.concatenate([d_gate, d_up, hidden])
        other = swap_core(mine)
        gradient = contract(mine[:2 * half], pair_keep, 0, 1) + contract(other[:2 * half], pair_send, 0, 1)
        gradient = gradient.astype(BF) if group[0][1] else gradient
        for i, (s, k) in enumerate(group):
            partial[s][k] = gradient[i * size:(i + 1) * size]
        low = jnp.where(core == 0, mine, other)
        high = jnp.where(core == 0, other, mine)
        d_gates.append(jnp.concatenate([low[:half], high[:half]]))
        d_ups.append(jnp.concatenate([low[half:2 * half], high[half:2 * half]]))
        hiddens.append(jnp.concatenate([low[2 * half:], high[2 * half:]]))

    results = []
    for stream, order in enumerate((("y", "x"), ("x", "y"))):
        total = scatter_first(partial[stream], order[0])
        results.append(scatter(total, order[1]))
    grad_input = scatter_slabs(results).astype(BF)

    ready = (partial[0][2], partial[1][2])
    (d_gates, d_ups, hiddens) = after((d_gates, d_ups, hiddens), ready)
    all_x = jnp.concatenate(xs)
    all_g = jnp.concatenate(gs)
    grad_gate = contract(jnp.concatenate(d_gates, axis=1), all_x, 1, 0).astype(BF).T
    grad_up = contract(jnp.concatenate(d_ups, axis=1), all_x, 1, 0).astype(BF).T
    grad_down = contract(jnp.concatenate(hiddens, axis=1), all_g, 1, 0).astype(BF)
    return (grad_input, grad_gate, grad_up, grad_down)


def solution(mesh):
    in_specs = (P("col", "row"), P("col", "row"), P("row", "col"), P("row", "col"), P("col", "row"))
    out_specs = (P("col", "row"), P("row", "col"), P("row", "col"), P("col", "row"))
    return jax.shard_map(local, mesh=mesh, in_specs=in_specs, out_specs=out_specs, check_vma=False)
```

```python
import jax
import jax.numpy as jnp
from jax import lax
from jax.sharding import PartitionSpec as P

BF = jnp.bfloat16
F32 = jnp.float32


def shift(value, axis, amount):
    def moved(c):
        y, z, x = c // 16, (c // 4) % 4, c % 4
        if axis == "y":
            y = (y + amount) % 4
        elif axis == "z":
            z = (z + amount) % 4
        else:
            x = (x + amount) % 4
        return y * 16 + z * 4 + x

    return lax.ppermute(value, "col", [(c, moved(c)) for c in range(64)])


def swap_core(value):
    return lax.ppermute(value, "row", [(r, r ^ 1) for r in range(4)])


def swap_chip(value):
    return lax.ppermute(value, "row", [(r, r ^ 2) for r in range(4)])


def contract(left, right, left_dim, right_dim):
    return lax.dot_general(
        left, right, (((left_dim,), (right_dim,)), ((), ())), preferred_element_type=F32
    )


def pointwise(gate, up, hidden_grad):
    logistic = jax.nn.sigmoid(gate)
    active = gate * logistic
    hidden = (active * up).astype(BF)
    d_gate = (hidden_grad * up * logistic * (1.0 + gate * (1.0 - logistic))).astype(BF)
    d_up = (hidden_grad * active).astype(BF)
    return hidden, d_gate, d_up


def gather_block(parts, axis):
    pieces = [parts] + [shift(parts, axis, -k) for k in (1, 2, 3)]
    return jnp.stack(pieces, axis=1)


def gather_last(own, axis):
    down = shift(own, axis, 1)
    up = shift(own, axis, -1)
    far = (shift(down[0], axis, 1), shift(up[1], axis, -1))
    return {0: (own[0], own[1]), -1: (down[0], down[1]), 1: (up[0], up[1]), 2: far}


def scatter_first(blocks, axis):
    total = blocks[0]
    for k in (1, -1, 2):
        total = total + shift(blocks[k], axis, k).astype(F32)
    return total


def scatter(total, axis):
    rows = total.shape[0] // 4
    result = total[:rows]
    for k in (1, 3, 2):
        result = result + shift(total[k * rows:(k + 1) * rows].astype(BF), axis, k).astype(F32)
    return result


def scatter_slabs(totals):
    rows = totals[0].shape[0] // 4
    pieces = [jnp.concatenate([t[k * rows:(k + 1) * rows] for t in totals]) for k in range(4)]
    result = pieces[0]
    for k in (1, 3, 2):
        result = result + shift(pieces[k].astype(BF), "z", k).astype(F32)
    return result


def after(values, earlier):
    return lax.optimization_barrier((values, earlier))[0]


def local(tokens, out_grad, gate_weight, up_weight, down_weight):
    width, hidden_units = gate_weight.shape
    half = hidden_units // 2
    core = lax.axis_index("row") % 2

    def halves(weight, dim):
        keep = lax.dynamic_slice_in_dim(weight, core * half, half, dim)
        send = lax.dynamic_slice_in_dim(weight, (1 - core) * half, half, dim)
        return keep, send

    gate_keep, gate_send = halves(gate_weight, 1)
    up_keep, up_send = halves(up_weight, 1)
    down_keep, down_send = halves(down_weight, 0)
    pair_keep = jnp.concatenate([gate_keep, up_keep], axis=1)
    pair_send = jnp.concatenate([gate_send, up_send], axis=1)

    rows = tokens.shape[0] // 2
    both = jnp.stack([tokens, out_grad])
    slabs = [both] + [shift(both, "z", -k) for k in (1, 2, 3)]
    slabs, weights = lax.optimization_barrier((slabs, (pair_keep, pair_send, down_keep, down_send)))
    pair_keep, pair_send, down_keep, down_send = weights
    blocks = {}
    for stream, (first, last) in enumerate((("x", "y"), ("y", "x"))):
        parts = jnp.stack([slab[:, stream * rows:(stream + 1) * rows] for slab in slabs], axis=1)
        whole = gather_block(parts, first).reshape(2, 16 * rows, width)
        blocks[stream] = gather_last(whole, last)
    size = 16 * rows

    groups = [[(0, 0), (1, 0)], [(1, -1), (1, 1)], [(0, -1), (0, 1)], [(0, 2), (1, 2)]]
    xs, gs, hiddens, d_gates, d_ups = [], [], [], [], []
    partial = {0: {}, 1: {}}
    states = []
    for group in groups:
        x = jnp.concatenate([blocks[s][k][0] for s, k in group])
        g = jnp.concatenate([blocks[s][k][1] for s, k in group])
        if states:
            x, g = after((x, g), states[-1][1])
        xs.append(x)
        gs.append(g)
        got_pair = swap_core(contract(pair_send, x, 0, 1))
        got_grad = swap_core(contract(down_send, g, 1, 1))
        sum_pair = contract(pair_keep, x, 0, 1) + got_pair
        sum_grad = contract(down_keep, g, 1, 1) + got_grad
        sums = jnp.concatenate([sum_pair, sum_grad])
        states.append([sums, sums.astype(BF)])
    for group, (sums, sent) in zip(groups, states):
        sums = sums + swap_chip(sent).astype(F32)
        hidden, d_gate, d_up = pointwise(sums[:half], sums[half:2 * half], sums[2 * half:])
        mine = jnp.concatenate([d_gate, d_up, hidden])
        other = swap_core(mine)
        gradient = contract(mine[:2 * half], pair_keep, 0, 1) + contract(other[:2 * half], pair_send, 0, 1)
        gradient = gradient.astype(BF) if group[0][1] else gradient
        for i, (s, k) in enumerate(group):
            partial[s][k] = gradient[i * size:(i + 1) * size]
        low = jnp.where(core == 0, mine, other)
        high = jnp.where(core == 0, other, mine)
        d_gates.append(jnp.concatenate([low[:half], high[:half]]))
        d_ups.append(jnp.concatenate([low[half:2 * half], high[half:2 * half]]))
        hiddens.append(jnp.concatenate([low[2 * half:], high[2 * half:]]))

    results = []
    for stream, order in enumerate((("y", "x"), ("x", "y"))):
        total = scatter_first(partial[stream], order[0])
        results.append(scatter(total, order[1]))
    grad_input = scatter_slabs(results).astype(BF)

    ready = (partial[0][2], partial[1][2])
    (d_gates, d_ups, hiddens) = after((d_gates, d_ups, hiddens), ready)
    all_x = jnp.concatenate(xs)
    all_g = jnp.concatenate(gs)
    grad_gate = contract(jnp.concatenate(d_gates, axis=1), all_x, 1, 0).astype(BF).T
    grad_up = contract(jnp.concatenate(d_ups, axis=1), all_x, 1, 0).astype(BF).T
    grad_down = contract(jnp.concatenate(hiddens, axis=1), all_g, 1, 0).astype(BF)
    return (grad_input, grad_gate, grad_up, grad_down)


def solution(mesh):
    in_specs = (P("col", "row"), P("col", "row"), P("row", "col"), P("row", "col"), P("col", "row"))
    out_specs = (P("col", "row"), P("row", "col"), P("row", "col"), P("col", "row"))
    return jax.shard_map(local, mesh=mesh, in_specs=in_specs, out_specs=out_specs, check_vma=False)
```

```python
import jax
import jax.numpy as jnp
from jax import lax
from jax.sharding import PartitionSpec as P

BF = jnp.bfloat16
F32 = jnp.float32


def shift(value, axis, amount):
    def moved(c):
        y, z, x = c // 16, (c // 4) % 4, c % 4
        if axis == "y":
            y = (y + amount) % 4
        elif axis == "z":
            z = (z + amount) % 4
        else:
            x = (x + amount) % 4
        return y * 16 + z * 4 + x

    return lax.ppermute(value, "col", [(c, moved(c)) for c in range(64)])


def swap_core(value):
    return lax.ppermute(value, "row", [(r, r ^ 1) for r in range(4)])


def swap_chip(value):
    return lax.ppermute(value, "row", [(r, r ^ 2) for r in range(4)])


def contract(left, right, left_dim, right_dim):
    return lax.dot_general(
        left, right, (((left_dim,), (right_dim,)), ((), ())), preferred_element_type=F32
    )


def pointwise(gate, up, hidden_grad):
    logistic = jax.nn.sigmoid(gate)
    active = gate * logistic
    hidden = (active * up).astype(BF)
    d_gate = (hidden_grad * up * logistic * (1.0 + gate * (1.0 - logistic))).astype(BF)
    d_up = (hidden_grad * active).astype(BF)
    return hidden, d_gate, d_up


def gather_block(parts, axis):
    pieces = [parts] + [shift(parts, axis, -k) for k in (1, 2, 3)]
    return jnp.stack(pieces, axis=1)


def gather_last(own, axis):
    down = shift(own, axis, 1)
    up = shift(own, axis, -1)
    far = (shift(down[0], axis, 1), shift(up[1], axis, -1))
    return {0: (own[0], own[1]), -1: (down[0], down[1]), 1: (up[0], up[1]), 2: far}


def scatter_first(blocks, axis):
    total = blocks[0]
    for k in (1, -1, 2):
        total = total + shift(blocks[k], axis, k).astype(F32)
    return total


def scatter(total, axis):
    rows = total.shape[0] // 4
    result = total[:rows]
    for k in (1, 3, 2):
        result = result + shift(total[k * rows:(k + 1) * rows].astype(BF), axis, k).astype(F32)
    return result


def scatter_slabs(totals):
    rows = totals[0].shape[0] // 4
    pieces = [jnp.concatenate([t[k * rows:(k + 1) * rows] for t in totals]) for k in range(4)]
    result = pieces[0]
    for k in (1, 3, 2):
        result = result + shift(pieces[k].astype(BF), "z", k).astype(F32)
    return result


def after(values, earlier):
    return lax.optimization_barrier((values, earlier))[0]


def local(tokens, out_grad, gate_weight, up_weight, down_weight):
    width, hidden_units = gate_weight.shape
    half = hidden_units // 2
    core = lax.axis_index("row") % 2

    def halves(weight, dim):
        keep = lax.dynamic_slice_in_dim(weight, core * half, half, dim)
        send = lax.dynamic_slice_in_dim(weight, (1 - core) * half, half, dim)
        return keep, send

    gate_keep, gate_send = halves(gate_weight, 1)
    up_keep, up_send = halves(up_weight, 1)
    down_keep, down_send = halves(down_weight, 0)
    pair_keep = jnp.concatenate([gate_keep, up_keep], axis=1)
    pair_send = jnp.concatenate([gate_send, up_send], axis=1)

    rows = tokens.shape[0] // 2
    both = jnp.stack([tokens, out_grad])
    slabs = [both] + [shift(both, "z", -k) for k in (1, 2, 3)]
    slabs, weights = lax.optimization_barrier((slabs, (pair_keep, pair_send, down_keep, down_send)))
    pair_keep, pair_send, down_keep, down_send = weights
    blocks = {}
    for stream, (first, last) in enumerate((("x", "y"), ("y", "x"))):
        parts = jnp.stack([slab[:, stream * rows:(stream + 1) * rows] for slab in slabs], axis=1)
        whole = gather_block(parts, first).reshape(2, 16 * rows, width)
        blocks[stream] = gather_last(whole, last)
    size = 16 * rows

    groups = [[(0, 0), (1, 0)], [(1, -1), (1, 1)], [(0, -1), (0, 1)], [(0, 2), (1, 2)]]
    xs, gs, hiddens, d_gates, d_ups = [], [], [], [], []
    partial = {0: {}, 1: {}}
    states = []
    for group in groups:
        x = jnp.concatenate([blocks[s][k][0] for s, k in group])
        g = jnp.concatenate([blocks[s][k][1] for s, k in group])
        if states:
            x, g = after((x, g), states[-1][1])
        xs.append(x)
        gs.append(g)
        got_pair = swap_core(contract(pair_send, x, 0, 1))
        got_grad = swap_core(contract(down_send, g, 1, 1))
        sum_pair = contract(pair_keep, x, 0, 1) + got_pair
        sum_grad = contract(down_keep, g, 1, 1) + got_grad
        sums = jnp.concatenate([sum_pair, sum_grad])
        states.append([sums, sums.astype(BF)])
    for group, (sums, sent) in zip(groups, states):
        sums = sums + swap_chip(sent).astype(F32)
        hidden, d_gate, d_up = pointwise(sums[:half], sums[half:2 * half], sums[2 * half:])
        mine = jnp.concatenate([d_gate, d_up, hidden])
        other = swap_core(mine)
        gradient = contract(mine[:2 * half], pair_keep, 0, 1) + contract(other[:2 * half], pair_send, 0, 1)
        gradient = gradient.astype(BF) if group[0][1] else gradient
        for i, (s, k) in enumerate(group):
            partial[s][k] = gradient[i * size:(i + 1) * size]
        low = jnp.where(core == 0, mine, other)
        high = jnp.where(core == 0, other, mine)
        d_gates.append(jnp.concatenate([low[:half], high[:half]]))
        d_ups.append(jnp.concatenate([low[half:2 * half], high[half:2 * half]]))
        hiddens.append(jnp.concatenate([low[2 * half:], high[2 * half:]]))

    results, totals = [], []
    for stream, order in enumerate((("y", "x"), ("x", "y"))):
        total = scatter_first(partial[stream], order[0])
        totals.append(total)
        results.append(scatter(total, order[1]))
    grad_input = scatter_slabs(results).astype(BF)

    d_gates, d_ups, hiddens = after((d_gates, d_ups, hiddens), totals[1])
    all_x = jnp.concatenate(xs)
    all_g = jnp.concatenate(gs)
    grad_gate = contract(jnp.concatenate(d_gates, axis=1), all_x, 1, 0).astype(BF).T
    grad_up = contract(jnp.concatenate(d_ups, axis=1), all_x, 1, 0).astype(BF).T
    grad_down = contract(jnp.concatenate(hiddens, axis=1), all_g, 1, 0).astype(BF)
    return (grad_input, grad_gate, grad_up, grad_down)


def solution(mesh):
    in_specs = (P("col", "row"), P("col", "row"), P("row", "col"), P("row", "col"), P("col", "row"))
    out_specs = (P("col", "row"), P("row", "col"), P("row", "col"), P("col", "row"))
    return jax.shard_map(local, mesh=mesh, in_specs=in_specs, out_specs=out_specs, check_vma=False)
```
